512 devices in a mesh: pair: 64 (over z, x), int: 8 (over y, core).
Axes of the slice: x: 4, y: 4, z: 16, core: 2. Of those that a mesh axis runs over, the one named last changes fastest.
Arguments:
- amps: bfloat16 [512, 64, 4096], P('pair', None, 'int'), may hold values from -6 to 6
- amp_mask: int32 [512, 64], P('pair'), may hold values 0 or 1
- integrals: bfloat16 [64, 4096, 4096], P('pair', None, 'int'), may hold values from -0.09375 to 0.09375
- block_mask: int32 [64], P('pair'), may hold values 0 or 1
- in_tiles: int32 [64], replicated, may hold values from 0 to 63, each once
- out_tiles: int32 [64], replicated, may hold values from 0 to 63, each once
- vir_energy: float32 [1024], replicated, may hold values from 0.5 to 3
- pair_energy: float32 [512], P('pair'), may hold values from -4 to -1
- dressing: bfloat16 [1024, 1024], P('pair'), may hold values from -0.1875 to 0.1875
Outputs:
- new_amps: bfloat16 [512, 64, 4096], P('pair', None, 'int')
The draws below stay inside these ranges and needn't reach their ends.
Inputs may be any that keep to these rules, and one draw needn't show every extreme that they name: `in_tiles`: a permutation of the 64 tiles. `out_tiles`: a permutation of the 64 tiles.
All inputs are finite; a program needn't handle non-finite values. No bound on the sum of `amp_mask` or of `block_mask` on one device may be relied on, other than what follows from the above.
Results may differ from the reference program's by a relative error of at most 0.0038.
Values may be sent and summed in bfloat16 or wider, within the bound.
A program may use at most 64 MiB of HBM per device.

```python
import jax
import jax.numpy as jnp
from jax import lax

TILE = 64
VT = 16
WA = 4
P_SIZE = 512
NPT = 64
TE = 4096
NV = 1024
N_INT = 8


def place_ends(array, key, smallest, largest):
    longest = array.shape.index(max(array.shape))
    spots = []
    for shift in (0, 1):
        where = [jax.random.randint(jax.random.fold_in(key, axis), (), 0, length) for axis, length in enumerate(array.shape)]
        where[longest] = (where[longest] + shift) % array.shape[longest]
        spots.append(tuple(where))
    return array.at[spots[0]].set(smallest).at[spots[1]].set(largest)


def level_of(own_key, shape, pieces, least, top_value):
    level, own = 1.0, jax.random.fold_in(own_key, 6)
    for position, parts in pieces:
        steps = jnp.exp(jax.random.uniform(jax.random.fold_in(own, position), (parts,), jnp.float32, least / len(pieces), top_value / len(pieces)))
        level = level * jnp.repeat(steps, shape[position] // parts).reshape([-1 if axis == position else 1 for axis in range(len(shape))])
    return level


def gaussian(rng, dims, scale, reach, split=(), kind=jnp.bfloat16):
    result = scale * jax.random.normal(rng, dims, jnp.float32)
    if split:
        result = result * level_of(rng, dims, split, -0.22, 0.18)
    return jnp.clip(result, -reach, reach).astype(kind)


def setup_inputs(seed: int = 0) -> dict:
    splits = jax.random.split(jax.random.key(seed), 10)
    return {
        "amps": gaussian(splits[0], (P_SIZE, NPT, TE), 1.0, 6.0, ((0, 64), (2, 8))),
        "amp_mask": place_ends((jax.random.randint(splits[1], (P_SIZE, NPT), 0, 4) < 3).astype(jnp.int32), jax.random.fold_in(splits[1], 1), 0, 1),
        "integrals": gaussian(splits[2], (NPT, TE, TE), TE ** -0.5, 0.09375, ((0, 64), (2, 8))),
        "block_mask": place_ends((jax.random.randint(splits[3], (NPT,), 0, 4) < 3).astype(jnp.int32), jax.random.fold_in(splits[3], 1), 0, 1),
        "in_tiles": jax.random.permutation(splits[4], NPT).astype(jnp.int32),
        "out_tiles": jax.random.permutation(splits[5], NPT).astype(jnp.int32),
        "vir_energy": jnp.clip(jax.random.uniform(splits[6], (NV,), jnp.float32, 0.5, 3.0), 0.5, 3.0),
        "pair_energy": jnp.clip(-4.0 + 3.0 * jax.random.uniform(splits[7], (P_SIZE,), jnp.float32) ** level_of(splits[7], (P_SIZE,), ((0, 64),), -0.2, 0.2), -4.0, -1.0),
        "dressing": gaussian(splits[8], (NV, NV), NV ** -0.5, 0.1875, ((0, 64),)),
    }


def reference(amps, amp_mask, integrals, block_mask, in_tiles, out_tiles, vir_energy, pair_energy, dressing):
    pair_count = amps.shape[0]
    tile_count = amps.shape[1]
    tile_entries = amps.shape[2]
    group_size = tile_entries // N_INT
    masked = jnp.where(amp_mask[:, :, None] > 0, amps, jnp.zeros_like(amps))

    def one_slot(slot_args):
        integral_block, source, keep_block = slot_args
        amp_rows = jnp.take(masked, source.astype(jnp.int32), axis=1).astype(jnp.float32)
        amp_rows = amp_rows.reshape(pair_count, N_INT, group_size)
        block_wide = integral_block.astype(jnp.float32).reshape(tile_entries, N_INT, group_size)
        int_parts = jnp.einsum("pnk,ank->npa", amp_rows, block_wide)
        int_parts = int_parts * keep_block.astype(jnp.float32)
        int_parts = lax.optimization_barrier(int_parts.astype(jnp.bfloat16)).astype(jnp.float32)
        return jnp.sum(int_parts, axis=0)

    ladder_slots = lax.map(one_slot, (integrals, in_tiles, block_mask))
    slot_of = jnp.zeros((tile_count,), jnp.int32).at[out_tiles.astype(jnp.int32)].set(jnp.arange(tile_count, dtype=jnp.int32))
    ladder = jnp.transpose(jnp.take(ladder_slots, slot_of, axis=0), (1, 0, 2))

    amp_grid = masked.reshape(pair_count, WA, VT, TILE, TILE).astype(jnp.float32)
    dress_grid = dressing.reshape(VT, TILE, VT, TILE).astype(jnp.float32)
    cycle = jnp.einsum("pxyuv,yvzw->pxzuw", amp_grid, dress_grid).reshape(pair_count, tile_count, tile_entries)

    energies = vir_energy.reshape(VT, TILE)
    first_energy = energies[:WA]
    denominator = pair_energy[:, None, None, None, None] - first_energy[None, :, None, :, None] - energies[None, None, :, None, :]
    denominator = denominator.reshape(pair_count, tile_count, tile_entries)
    updated = masked.astype(jnp.float32) + (ladder + cycle) / denominator
    return updated.astype(jnp.bfloat16)
```

```python
import functools

import jax
import jax.numpy as jnp
from jax import lax
from jax.experimental import pallas as pl
from jax.experimental.pallas import tpu as pltpu
from jax.sharding import PartitionSpec as P

MESH = pl.DeviceIdType.MESH
BF16 = jnp.bfloat16
F32 = jnp.float32
WA = 4
NX = 4
LANES = 128
NC = 2
CUTS = (0, 44, 64)


def kernel(
    cuts,
    amps_ref,
    mask_ref,
    ints_hbm,
    block_s,
    in_s,
    slot_s,
    energy_s,
    energy_ref,
    pair_energy_s,
    dress_ref,
    out_ref,
    ints,
    amps32,
    asend,
    arecv,
    rows,
    psend,
    precv,
    own,
    ysend,
    yrecv,
    dsend,
    drecv,
    gathered,
    dress,
    lhs,
    cycle,
    ladder,
    first_energy,
    second_energy,
    ints_sem,
    a_send,
    a_recv,
    p_send,
    p_recv,
    y_send,
    y_recv,
    d_send,
    d_recv,
    g_send,
    g_recv,
):
    npair = asend.shape[0]
    pairs, tiles, share = amps_ref.shape
    nz = npair // NX
    nint, _, _, _, band = gathered.shape
    ny = nint // NC
    vt = tiles // WA
    chunks = len(cuts) - 1
    blocks = share // LANES
    n, i = lax.axis_index("pair"), lax.axis_index("int")
    z, x = lax.div(n, NX), lax.rem(n, NX)
    y, c = lax.div(i, NC), lax.rem(i, NC)

    def peer(o, sign):
        zi, dx = lax.div(o, NX), lax.rem(o, NX)
        half = lax.div(zi + 1, 2)
        dz = jnp.where(lax.rem(zi, 2) == 1, half, nz - half)
        zz = lax.rem(z + nz + sign * dz + nz, nz)
        xx = lax.rem(x + NX + sign * dx, NX)
        return zz * NX + xx

    def y_peer(dy):
        return lax.rem(y + dy, ny) * NC + c

    partner = y * NC + (1 - c)

    barrier = pltpu.get_barrier_semaphore()

    def greet(o, carry):
        pl.semaphore_signal(barrier, 1, device_id={"pair": peer(o, 1)}, device_id_type=MESH)
        return carry

    lax.fori_loop(1, npair, greet, 0)
    pl.semaphore_signal(barrier, 1, device_id={"int": partner}, device_id_type=MESH)
    for dy in range(1, ny):
        pl.semaphore_signal(barrier, 1, device_id={"int": y_peer(dy)}, device_id_type=MESH)

    load_ints = pltpu.make_async_copy(ints_hbm.at[0], ints, ints_sem)
    load_ints.start()

    mask_t = jnp.transpose(mask_ref[...].astype(F32))
    for p in range(pairs):
        keep = jnp.broadcast_to(mask_t[:, p : p + 1], (tiles, share)) > 0
        kept = jnp.where(keep, amps_ref[p].astype(F32), 0.0)
        for b in range(blocks):
            amps32[b, p * tiles : (p + 1) * tiles, :] = kept[:, b * LANES : (b + 1) * LANES]

    def order(o, carry):
        t = in_s[peer(o, 1)]
        for b in range(blocks):
            asend[o, :, b * LANES : (b + 1) * LANES] = amps32[b, pl.ds(t, pairs, stride=tiles), :].astype(BF16)
        return carry

    lax.fori_loop(0, npair, order, 0)
    arecv[0] = asend[0]

    pl.semaphore_wait(barrier, npair - 1 + 1 + ny - 1)

    def a_copy(k, o):
        return pltpu.make_async_remote_copy(
            asend.at[o], arecv.at[o], a_send.at[k], a_recv.at[k],
            device_id={"pair": peer(o, 1)}, device_id_type=MESH)

    def many(src, dst, ssem, rsem, k):
        first, last = max(cuts[k], 1), cuts[k + 1]
        return pltpu.make_async_remote_copy(
            src.at[pl.ds(first, last - first)], dst.at[pl.ds(first, last - first)],
            ssem.at[k], rsem.at[k], device_id={"pair": peer(1, 1)}, device_id_type=MESH)

    for k in range(chunks):
        def start_a(o, carry, k=k):
            a_copy(k, o).start()
            return carry
        lax.fori_loop(max(cuts[k], 1), cuts[k + 1], start_a, 0)

    piece = dress_ref.at[:, pl.ds(pl.multiple_of(i * band, band), band)]
    own_piece = pltpu.make_async_copy(piece, gathered.at[i, x, z], g_send.at[0])
    own_piece.start()
    own_piece.wait()

    def g_z_copy(dz):
        return pltpu.make_async_remote_copy(
            piece, gathered.at[i, x, z], g_send.at[1], g_recv.at[1],
            device_id={"pair": lax.rem(z + dz, nz) * NX + x}, device_id_type=MESH)

    def g_x_copy(dx):
        return pltpu.make_async_remote_copy(
            gathered.at[i, x], gathered.at[i, x], g_send.at[2], g_recv.at[2],
            device_id={"pair": z * NX + lax.rem(x + dx, NX)}, device_id_type=MESH)

    def g_y_copy(dy):
        return pltpu.make_async_remote_copy(
            gathered.at[i], gathered.at[i], g_send.at[3], g_recv.at[3],
            device_id={"int": y_peer(dy)}, device_id_type=MESH)

    def g_c_copy(yy):
        return pltpu.make_async_remote_copy(
            gathered.at[yy * NC + c], gathered.at[yy * NC + c], g_send.at[4], g_recv.at[4],
            device_id={"int": partner}, device_id_type=MESH)

    def start_gz(dz, carry):
        g_z_copy(dz).start()
        return carry

    lax.fori_loop(1, nz, start_gz, 0)

    def drain(ref, ssem, rsem):
        copy = pltpu.make_async_remote_copy(
            ref, ref, ssem, rsem, device_id={"int": partner}, device_id_type=MESH)
        copy.wait_send()
        copy.wait_recv()

    low = lax.broadcasted_iota(jnp.int32, (1, 128), 1) < 64
    count = pairs * WA
    for j in range(vt // 2):
        for ap in range(blocks):
            even = amps32[ap, pl.ds(2 * j, count, stride=vt), :]
            odd = amps32[ap, pl.ds(2 * j + 1, count, stride=vt), :]
            at = ap * count
            lhs[at : at + count, j * 128 : (j + 1) * 128] = jnp.where(
                low, even, pltpu.roll(odd, 64, 1)).astype(BF16)
            at += blocks * count
            lhs[at : at + count, j * 128 : (j + 1) * 128] = jnp.where(
                low, pltpu.roll(even, 64, 1), odd).astype(BF16)

    energies = energy_ref[...]
    turned = pltpu.roll(energies, 64, 1)
    for j in range(vt // 2):
        spread = jnp.where(low, energies[j : j + 1], turned[j : j + 1])
        second_energy[2 * j : 2 * j + 1, :] = jnp.concatenate([spread] * (share // 128), 1)
        spread = jnp.where(low, turned[j : j + 1], energies[j : j + 1])
        second_energy[2 * j + 1 : 2 * j + 2, :] = jnp.concatenate([spread] * (share // 128), 1)
    strip = lax.broadcasted_iota(jnp.int32, (1, share), 1) // 64
    for a in range(WA):
        row = jnp.zeros((1, share), F32)
        for s in range(share // 64):
            row = jnp.where(strip == s, energy_s[64 * a + i * (share // 64) + s], row)
        first_energy[a : a + 1, :] = row

    scale = block_s[0].astype(F32)
    load_ints.wait()

    def product(r0, rn, j):
        block = ints[pl.ds(pl.multiple_of(j * share, share), share), :]
        part = lax.dot_general(
            rows[r0 : r0 + rn, :], block, (((1,), (1,)), ((), ())), preferred_element_type=F32)
        return (part * scale).astype(BF16)

    def p_copy(k, yy):
        span = pl.ds(cuts[k] * pairs, (cuts[k + 1] - cuts[k]) * pairs)
        return pltpu.make_async_remote_copy(
            psend.at[yy, span], precv.at[yy, span], p_send.at[k, yy], p_recv.at[k, yy],
            device_id={"int": partner}, device_id_type=MESH)

    def y_copy(k, dy):
        span = pl.ds(cuts[k] * pairs, (cuts[k + 1] - cuts[k]) * pairs)
        return pltpu.make_async_remote_copy(
            ysend.at[dy - 1, span], yrecv.at[dy - 1, span], y_send.at[k, dy - 1], y_recv.at[k, dy - 1],
            device_id={"int": y_peer(dy)}, device_id_type=MESH)

    def multiply(k):
        o0, o1 = cuts[k], cuts[k + 1]
        r0, rn = o0 * pairs, (o1 - o0) * pairs
        many(asend, arecv, a_send, a_recv, k).wait_recv()
        rows[r0 : r0 + rn, :] = arecv[o0:o1].astype(F32).reshape(rn, share).astype(BF16)

        def for_partner(yy, carry):
            psend[yy, r0 : r0 + rn, :] = product(r0, rn, yy * NC + 1 - c)
            p_copy(k, yy).start()
            return carry

        lax.fori_loop(0, ny, for_partner, 0)

        def for_chip(step, carry):
            dy = ny - 1 - step
            yy = lax.rem(y + dy, ny)
            part = product(r0, rn, yy * NC + c).astype(F32)
            p_copy(k, yy).wait_recv()
            part = part + precv[yy, r0 : r0 + rn, :].astype(F32)

            @pl.when(dy > 0)
            def _():
                ysend[dy - 1, r0 : r0 + rn, :] = part.astype(BF16)
                y_copy(k, dy).start()

            @pl.when(dy == 0)
            def _():
                own[r0 : r0 + rn, :] = part

            return carry

        lax.fori_loop(0, ny, for_chip, 0)

    def d_copy(k, o):
        return pltpu.make_async_remote_copy(
            dsend.at[o], drecv.at[o], d_send.at[k], d_recv.at[k],
            device_id={"pair": peer(o, -1)}, device_id_type=MESH)

    def finish(k):
        o0, o1 = cuts[k], cuts[k + 1]
        r0, rn = o0 * pairs, (o1 - o0) * pairs
        total = own[r0 : r0 + rn, :]
        for dy in range(1, ny):
            y_copy(k, dy).wait_recv()
            total = total + yrecv[dy - 1, r0 : r0 + rn, :].astype(F32)
        dsend[o0:o1] = total.reshape(o1 - o0, pairs, share).astype(BF16)

        def start_d(o, carry):
            d_copy(k, o).start()
            return carry

        if o0 == 0:
            drecv[0] = dsend[0]
        lax.fori_loop(max(o0, 1), o1, start_d, 0)

    for k in range(chunks):
        multiply(k)
        if k == 0:
            drain(gathered.at[i, x, pl.ds(0, nz - 1)], g_send.at[1], g_recv.at[1])
            for dx in range(1, NX):
                g_x_copy(dx).start()
        if k == chunks - 1:
            drain(gathered.at[i, pl.ds(0, NX - 1)], g_send.at[2], g_recv.at[2])
            for dy in range(1, ny):
                g_y_copy(dy).start()
        if k > 0:
            finish(k - 1)
    finish(chunks - 1)

    drain(gathered.at[pl.ds(0, ny - 1)], g_send.at[3], g_recv.at[3])
    for yy in range(ny):
        g_c_copy(yy).start()
    drain(gathered.at[pl.ds(0, ny)], g_send.at[4], g_recv.at[4])

    for b in range(nint):
        for xx in range(NX):
            dress[:, xx, :, b * band : (b + 1) * band] = gathered[b, xx]
    width = dress.shape[-1]
    right = dress[...].reshape(width, width)
    result = jnp.dot(lhs[...], right, preferred_element_type=F32)
    for j in range(vt // 2):
        for ap in range(blocks):
            at = ap * count
            first = result[at : at + count, j * 128 : (j + 1) * 128]
            at += blocks * count
            last = result[at : at + count, j * 128 : (j + 1) * 128]
            cycle[ap, pl.ds(2 * j, count, stride=vt), :] = jnp.where(low, first, pltpu.roll(last, 64, 1))
            cycle[ap, pl.ds(2 * j + 1, count, stride=vt), :] = jnp.where(low, pltpu.roll(first, 64, 1), last)

    for k in range(chunks):
        many(dsend, drecv, d_send, d_recv, k).wait_recv()

    def place(u, carry):
        q = slot_s[u]
        dz = lax.rem(lax.div(q, NX) - z + nz, nz)
        dx = lax.rem(lax.rem(q, NX) - x + NX, NX)
        zi = jnp.where(dz == 0, 0, jnp.where(2 * dz <= nz, 2 * dz - 1, 2 * (nz - dz)))
        block = drecv[zi * NX + dx].astype(F32)
        for b in range(blocks):
            ladder[b, pl.ds(u, pairs, stride=tiles), :] = block[:, b * LANES : (b + 1) * LANES]
        return carry

    lax.fori_loop(0, tiles, place, 0)

    def update(p, carry):
        for a in range(WA):
            at = pl.ds(pl.multiple_of(p * tiles + a * vt, vt), vt)
            below = (pair_energy_s[p] - first_energy[a : a + 1, :]) - second_energy[...]
            for b in range(blocks):
                lanes = slice(b * LANES, (b + 1) * LANES)
                value = amps32[b, at, :] + (ladder[b, at, :] + cycle[b, at, :]) / below[:, lanes]
                out_ref[p, a * vt : (a + 1) * vt, lanes] = value.astype(BF16)
        return carry

    lax.fori_loop(0, pairs, update, 0)

    for k in range(chunks):
        many(asend, arecv, a_send, a_recv, k).wait_send()
        many(dsend, drecv, d_send, d_recv, k).wait_send()
        for yy in range(ny):
            p_copy(k, yy).wait_send()
        for dy in range(1, ny):
            y_copy(k, dy).wait_send()


def shards(
    cuts, amps, amp_mask, integrals, block_mask, in_tiles, out_tiles, vir_energy, pair_energy, dressing
):
    pairs, tiles, share = amps.shape
    npair = tiles
    nz = npair // NX
    nint = integrals.shape[1] // share
    ny = nint // NC
    width = dressing.shape[1]
    chunks = len(cuts) - 1
    every = jnp.arange(tiles, dtype=jnp.int32)
    slot_of = jnp.sum(jnp.where(out_tiles[None, :] == every[:, None], every[None, :], 0), axis=1)
    vmem = pl.BlockSpec(memory_space=pltpu.VMEM)
    smem = pl.BlockSpec(memory_space=pltpu.SMEM)
    dma = pltpu.SemaphoreType.DMA
    total = npair * pairs
    return pl.pallas_call(
        functools.partial(kernel, cuts),
        out_shape=jax.ShapeDtypeStruct(amps.shape, BF16),
        in_specs=[vmem, vmem, pl.BlockSpec(memory_space=pl.ANY), smem, smem, smem, smem, vmem, smem, vmem],
        out_specs=vmem,
        scratch_shapes=[
            pltpu.VMEM((nint * share, share), BF16),
            pltpu.VMEM((share // LANES, pairs * tiles, LANES), F32),
            pltpu.VMEM((npair, pairs, share), BF16),
            pltpu.VMEM((npair, pairs, share), BF16),
            pltpu.VMEM((total, share), BF16),
            pltpu.VMEM((ny, total, share), BF16),
            pltpu.VMEM((ny, total, share), BF16),
            pltpu.VMEM((total, share), F32),
            pltpu.VMEM((ny - 1, total, share), BF16),
            pltpu.VMEM((ny - 1, total, share), BF16),
            pltpu.VMEM((npair, pairs, share), BF16),
            pltpu.VMEM((npair, pairs, share), BF16),
            pltpu.VMEM((nint, NX, nz, dressing.shape[0], width // nint), BF16),
            pltpu.VMEM((nz, NX, dressing.shape[0], width), BF16),
            pltpu.VMEM((pairs * WA * (share // 64), width), BF16),
            pltpu.VMEM((share // LANES, pairs * tiles, LANES), F32),
            pltpu.VMEM((share // LANES, pairs * tiles, LANES), F32),
            pltpu.VMEM((WA, share), F32),
            pltpu.VMEM((tiles // WA, share), F32),
            dma,
            dma((chunks,)),
            dma((chunks,)),
            dma((chunks, ny)),
            dma((chunks, ny)),
            dma((chunks, ny - 1)),
            dma((chunks, ny - 1)),
            dma((chunks,)),
            dma((chunks,)),
            dma((5,)),
            dma((5,)),
        ],
        compiler_params=pltpu.CompilerParams(collective_id=0, has_side_effects=True),
        name="ladder_update",
    )(
        amps, amp_mask, integrals, block_mask, in_tiles, slot_of, vir_energy,
        vir_energy.reshape(-1, 128), pair_energy, dressing,
    )


def solution(mesh):
    npair = mesh.shape["pair"]
    cuts = CUTS if npair == CUTS[-1] else (0, npair // 2, npair)
    in_specs = (
        P("pair", None, "int"),
        P("pair", None),
        P("pair", None, "int"),
        P("pair"),
        P(),
        P(),
        P(),
        P("pair"),
        P("pair", None),
    )
    out_specs = P("pair", None, "int")
    return jax.shard_map(
        functools.partial(shards, cuts), mesh=mesh, in_specs=in_specs, out_specs=out_specs, check_vma=False
    )
```

```python
import functools

import jax
import jax.numpy as jnp
from jax import lax
from jax.experimental import pallas as pl
from jax.experimental.pallas import tpu as pltpu
from jax.sharding import PartitionSpec as P

MESH = pl.DeviceIdType.MESH
BF16 = jnp.bfloat16
F32 = jnp.float32
WA = 4
NX = 4
LANES = 128
WINDOW = 2
LAG = 2
NC = 2


def kernel(
    cuts,
    amps_ref,
    mask_ref,
    ints_hbm,
    block_s,
    in_s,
    out_s,
    energy_s,
    energy_ref,
    pair_energy_s,
    dress_ref,
    out_ref,
    ints,
    amps32,
    asend,
    arecv,
    rows,
    psend,
    precv,
    own,
    ysend,
    yrecv,
    dsend,
    drecv,
    gathered,
    dress,
    lhs,
    cycle,
    ladder,
    placing,
    first_energy,
    second_energy,
    ints_sem,
    a_send,
    a_recv,
    p_send,
    p_recv,
    y_send,
    y_recv,
    d_send,
    d_recv,
    g_send,
    g_recv,
):
    npair = asend.shape[0]
    pairs, tiles, share = amps_ref.shape
    nz = npair // NX
    nint, _, _, _, band = gathered.shape
    ny = nint // NC
    vt = tiles // WA
    chunks = len(cuts) - 1
    blocks = share // LANES
    n, i = lax.axis_index("pair"), lax.axis_index("int")
    z, x = lax.div(n, NX), lax.rem(n, NX)
    y, c = lax.div(i, NC), lax.rem(i, NC)

    def peer(o, sign):
        dx, zi = lax.div(o, nz), lax.rem(o, nz)
        half = lax.div(zi + 1, 2)
        dz = jnp.where(lax.rem(zi, 2) == 1, half, nz - half)
        zz = lax.rem(z + nz + sign * dz + nz, nz)
        xx = lax.rem(x + NX + sign * dx, NX)
        return zz * NX + xx

    def far_first(first, last, body):
        lax.fori_loop(first, last, lambda s, carry: body(last - 1 - (s - first), carry), 0)

    def y_peer(dy):
        return lax.rem(y + dy, ny) * NC + c

    partner = y * NC + (1 - c)

    barrier = pltpu.get_barrier_semaphore()

    def greet(s, carry):
        zi, dx = nz - 1 - lax.div(s, NX), lax.rem(s, NX)
        pl.semaphore_signal(barrier, 1, device_id={"pair": peer(dx * nz + zi, 1)}, device_id_type=MESH)
        return carry

    lax.fori_loop(0, npair - NX, greet, 0)
    for dx in range(1, NX):
        pl.semaphore_signal(barrier, 1, device_id={"pair": peer(dx * nz, 1)}, device_id_type=MESH)
    pl.semaphore_signal(barrier, 1, device_id={"int": partner}, device_id_type=MESH)
    for dy in range(1, ny):
        pl.semaphore_signal(barrier, 1, device_id={"int": y_peer(dy)}, device_id_type=MESH)

    load_ints = pltpu.make_async_copy(ints_hbm.at[0], ints, ints_sem)
    load_ints.start()

    mask_t = jnp.transpose(mask_ref[...].astype(F32))
    for p in range(pairs):
        keep = jnp.broadcast_to(mask_t[:, p : p + 1], (tiles, share)) > 0
        kept = jnp.where(keep, amps_ref[p].astype(F32), 0.0)
        for b in range(blocks):
            amps32[b, p * tiles : (p + 1) * tiles, :] = kept[:, b * LANES : (b + 1) * LANES]

    def order(o, carry):
        t = in_s[peer(o, 1)]
        for b in range(blocks):
            asend[o, :, b * LANES : (b + 1) * LANES] = amps32[b, pl.ds(t, pairs, stride=tiles), :].astype(BF16)
        return carry

    lax.fori_loop(0, npair, order, 0)
    arecv[0] = asend[0]

    pl.semaphore_wait(barrier, npair - 1 + 1 + ny - 1)

    def a_copy(k, o):
        return pltpu.make_async_remote_copy(
            asend.at[o], arecv.at[o], a_send.at[k], a_recv.at[k],
            device_id={"pair": peer(o, 1)}, device_id_type=MESH)

    def many(src, dst, ssem, rsem, k):
        first, last = max(cuts[k], 1), cuts[k + 1]
        return pltpu.make_async_remote_copy(
            src.at[pl.ds(first, last - first)], dst.at[pl.ds(first, last - first)],
            ssem.at[k], rsem.at[k], device_id={"pair": peer(1, 1)}, device_id_type=MESH)

    def send_chunk(k):
        def start_a(o, carry):
            a_copy(k, o).start()
            return carry

        far_first(max(cuts[k], 1), cuts[k + 1], start_a)

    for k in range(min(WINDOW, chunks)):
        send_chunk(k)

    piece = dress_ref.at[:, pl.ds(pl.multiple_of(i * band, band), band)]
    own_piece = pltpu.make_async_copy(piece, gathered.at[i, x, z], g_send.at[0])
    own_piece.start()
    own_piece.wait()

    def g_z_copy(dz):
        return pltpu.make_async_remote_copy(
            piece, gathered.at[i, x, z], g_send.at[1], g_recv.at[1],
            device_id={"pair": lax.rem(z + dz, nz) * NX + x}, device_id_type=MESH)

    def g_x_copy(dx):
        return pltpu.make_async_remote_copy(
            gathered.at[i, x], gathered.at[i, x], g_send.at[2], g_recv.at[2],
            device_id={"pair": z * NX + lax.rem(x + dx, NX)}, device_id_type=MESH)

    def g_y_copy(dy):
        return pltpu.make_async_remote_copy(
            gathered.at[i], gathered.at[i], g_send.at[3], g_recv.at[3],
            device_id={"int": y_peer(dy)}, device_id_type=MESH)

    def g_c_copy(yy):
        return pltpu.make_async_remote_copy(
            gathered.at[yy * NC + c], gathered.at[yy * NC + c], g_send.at[4], g_recv.at[4],
            device_id={"int": partner}, device_id_type=MESH)

    def start_gz(dz, carry):
        g_z_copy(dz).start()
        return carry

    lax.fori_loop(1, nz, start_gz, 0)

    def drain(ref, ssem, rsem):
        copy = pltpu.make_async_remote_copy(
            ref, ref, ssem, rsem, device_id={"int": partner}, device_id_type=MESH)
        copy.wait_send()
        copy.wait_recv()

    low = lax.broadcasted_iota(jnp.int32, (1, 128), 1) < 64
    count = pairs * WA
    for j in range(vt // 2):
        for ap in range(blocks):
            even = amps32[ap, pl.ds(2 * j, count, stride=vt), :]
            odd = amps32[ap, pl.ds(2 * j + 1, count, stride=vt), :]
            at = ap * count
            lhs[at : at + count, j * 128 : (j + 1) * 128] = jnp.where(
                low, even, pltpu.roll(odd, 64, 1)).astype(BF16)
            at += blocks * count
            lhs[at : at + count, j * 128 : (j + 1) * 128] = jnp.where(
                low, pltpu.roll(even, 64, 1), odd).astype(BF16)

    energies = energy_ref[...]
    turned = pltpu.roll(energies, 64, 1)
    for j in range(vt // 2):
        spread = jnp.where(low, energies[j : j + 1], turned[j : j + 1])
        second_energy[2 * j : 2 * j + 1, :] = jnp.concatenate([spread] * (share // 128), 1)
        spread = jnp.where(low, turned[j : j + 1], energies[j : j + 1])
        second_energy[2 * j + 1 : 2 * j + 2, :] = jnp.concatenate([spread] * (share // 128), 1)
    strip = lax.broadcasted_iota(jnp.int32, (1, share), 1) // 64
    for a in range(WA):
        row = jnp.zeros((1, share), F32)
        for s in range(share // 64):
            row = jnp.where(strip == s, energy_s[64 * a + i * (share // 64) + s], row)
        first_energy[a : a + 1, :] = row

    column = lax.broadcasted_iota(jnp.int32, (1, npair * pairs), 1)
    owner = lax.div(column, pairs)

    def target(o, found):
        return jnp.where(owner == o, out_s[peer(o, 1)], found)

    row = lax.fori_loop(0, npair, target, jnp.zeros_like(column)) + lax.rem(column, pairs) * tiles
    for p in range(pairs):
        own_rows = lax.broadcasted_iota(jnp.int32, (tiles, npair * pairs), 0) + p * tiles
        placing[p * tiles : (p + 1) * tiles, :] = jnp.where(own_rows == row, 1.0, 0.0).astype(BF16)

    scale = block_s[0].astype(F32)
    load_ints.wait()

    def product(r0, rn, j):
        block = ints[pl.ds(pl.multiple_of(j * share, share), share), :]
        part = lax.dot_general(
            rows[r0 : r0 + rn, :], block, (((1,), (1,)), ((), ())), preferred_element_type=F32)
        return (part * scale).astype(BF16)

    def p_copy(k, yy):
        span = pl.ds(cuts[k] * pairs, (cuts[k + 1] - cuts[k]) * pairs)
        return pltpu.make_async_remote_copy(
            psend.at[yy, span], precv.at[yy, span], p_send.at[k, yy], p_recv.at[k, yy],
            device_id={"int": partner}, device_id_type=MESH)

    def y_copy(k, dy):
        span = pl.ds(cuts[k] * pairs, (cuts[k + 1] - cuts[k]) * pairs)
        return pltpu.make_async_remote_copy(
            ysend.at[dy - 1, span], yrecv.at[dy - 1, span], y_send.at[k, dy - 1], y_recv.at[k, dy - 1],
            device_id={"int": y_peer(dy)}, device_id_type=MESH)

    def multiply(k):
        o0, o1 = cuts[k], cuts[k + 1]
        r0, rn = o0 * pairs, (o1 - o0) * pairs
        many(asend, arecv, a_send, a_recv, k).wait_recv()
        if k + WINDOW < chunks:
            send_chunk(k + WINDOW)
        rows[r0 : r0 + rn, :] = arecv[o0:o1].astype(F32).reshape(rn, share).astype(BF16)

        def for_partner(yy, carry):
            psend[yy, r0 : r0 + rn, :] = product(r0, rn, yy * NC + 1 - c)
            p_copy(k, yy).start()
            return carry

        lax.fori_loop(0, ny, for_partner, 0)

        def for_chip(step, carry):
            dy = ny - 1 - step
            yy = lax.rem(y + dy, ny)
            part = product(r0, rn, yy * NC + c).astype(F32)
            p_copy(k, yy).wait_recv()
            part = part + precv[yy, r0 : r0 + rn, :].astype(F32)

            @pl.when(dy > 0)
            def _():
                ysend[dy - 1, r0 : r0 + rn, :] = part.astype(BF16)
                y_copy(k, dy).start()

            @pl.when(dy == 0)
            def _():
                own[r0 : r0 + rn, :] = part

            return carry

        lax.fori_loop(0, ny, for_chip, 0)

    def d_copy(k, o):
        return pltpu.make_async_remote_copy(
            dsend.at[o], drecv.at[o], d_send.at[k], d_recv.at[k],
            device_id={"pair": peer(o, -1)}, device_id_type=MESH)

    def finish(k):
        o0, o1 = cuts[k], cuts[k + 1]
        r0, rn = o0 * pairs, (o1 - o0) * pairs
        total = own[r0 : r0 + rn, :]
        for dy in range(1, ny):
            y_copy(k, dy).wait_recv()
            total = total + yrecv[dy - 1, r0 : r0 + rn, :].astype(F32)
        dsend[o0:o1] = total.reshape(o1 - o0, pairs, share).astype(BF16)

        def start_d(o, carry):
            d_copy(k, o).start()
            return carry

        if o0 == 0:
            drecv[0] = dsend[0]
        far_first(max(o0, 1), o1, start_d)

    for k in range(chunks):
        multiply(k)
        if k == 0:
            drain(gathered.at[i, x, pl.ds(0, nz - 1)], g_send.at[1], g_recv.at[1])
            for dx in range(1, NX):
                g_x_copy(dx).start()
        if k == chunks - 1:
            drain(gathered.at[i, pl.ds(0, NX - 1)], g_send.at[2], g_recv.at[2])
            for dy in range(1, ny):
                g_y_copy(dy).start()
        if k >= LAG:
            finish(k - LAG)
    for k in range(max(chunks - LAG, 0), chunks):
        finish(k)

    drain(gathered.at[pl.ds(0, ny - 1)], g_send.at[3], g_recv.at[3])
    for yy in range(ny):
        g_c_copy(yy).start()
    drain(gathered.at[pl.ds(0, ny)], g_send.at[4], g_recv.at[4])

    for b in range(nint):
        for xx in range(NX):
            dress[:, xx, :, b * band : (b + 1) * band] = gathered[b, xx]
    width = dress.shape[-1]
    right = dress[...].reshape(width, width)
    result = jnp.dot(lhs[...], right, preferred_element_type=F32)
    for j in range(vt // 2):
        for ap in range(blocks):
            at = ap * count
            first = result[at : at + count, j * 128 : (j + 1) * 128]
            at += blocks * count
            last = result[at : at + count, j * 128 : (j + 1) * 128]
            cycle[ap, pl.ds(2 * j, count, stride=vt), :] = jnp.where(low, first, pltpu.roll(last, 64, 1))
            cycle[ap, pl.ds(2 * j + 1, count, stride=vt), :] = jnp.where(low, pltpu.roll(first, 64, 1), last)

    for k in range(chunks):
        o0, o1 = cuts[k], cuts[k + 1]
        many(dsend, drecv, d_send, d_recv, k).wait_recv()
        block = drecv[o0:o1].astype(F32).reshape((o1 - o0) * pairs, share).astype(BF16)
        part = jnp.dot(placing[:, o0 * pairs : o1 * pairs], block, preferred_element_type=F32)
        ladder[...] = part if k == 0 else ladder[...] + part

    def update(p, carry):
        for a in range(WA):
            at = pl.ds(pl.multiple_of(p * tiles + a * vt, vt), vt)
            below = (pair_energy_s[p] - first_energy[a : a + 1, :]) - second_energy[...]
            for b in range(blocks):
                lanes = slice(b * LANES, (b + 1) * LANES)
                value = amps32[b, at, :] + (ladder[at, lanes] + cycle[b, at, :]) / below[:, lanes]
                out_ref[p, a * vt : (a + 1) * vt, lanes] = value.astype(BF16)
        return carry

    lax.fori_loop(0, pairs, update, 0)

    for k in range(chunks):
        many(asend, arecv, a_send, a_recv, k).wait_send()
        many(dsend, drecv, d_send, d_recv, k).wait_send()
        for yy in range(ny):
            p_copy(k, yy).wait_send()
        for dy in range(1, ny):
            y_copy(k, dy).wait_send()


def shards(
    cuts, amps, amp_mask, integrals, block_mask, in_tiles, out_tiles, vir_energy, pair_energy, dressing
):
    pairs, tiles, share = amps.shape
    npair = tiles
    nz = npair // NX
    nint = integrals.shape[1] // share
    ny = nint // NC
    width = dressing.shape[1]
    chunks = len(cuts) - 1
    vmem = pl.BlockSpec(memory_space=pltpu.VMEM)
    smem = pl.BlockSpec(memory_space=pltpu.SMEM)
    dma = pltpu.SemaphoreType.DMA
    total = npair * pairs
    return pl.pallas_call(
        functools.partial(kernel, cuts),
        out_shape=jax.ShapeDtypeStruct(amps.shape, BF16),
        in_specs=[vmem, vmem, pl.BlockSpec(memory_space=pl.ANY), smem, smem, smem, smem, vmem, smem, vmem],
        out_specs=vmem,
        scratch_shapes=[
            pltpu.VMEM((nint * share, share), BF16),
            pltpu.VMEM((share // LANES, pairs * tiles, LANES), F32),
            pltpu.VMEM((npair, pairs, share), BF16),
            pltpu.VMEM((npair, pairs, share), BF16),
            pltpu.VMEM((total, share), BF16),
            pltpu.VMEM((ny, total, share), BF16),
            pltpu.VMEM((ny, total, share), BF16),
            pltpu.VMEM((total, share), F32),
            pltpu.VMEM((ny - 1, total, share), BF16),
            pltpu.VMEM((ny - 1, total, share), BF16),
            pltpu.VMEM((npair, pairs, share), BF16),
            pltpu.VMEM((npair, pairs, share), BF16),
            pltpu.VMEM((nint, NX, nz, dressing.shape[0], width // nint), BF16),
            pltpu.VMEM((nz, NX, dressing.shape[0], width), BF16),
            pltpu.VMEM((pairs * WA * (share // 64), width), BF16),
            pltpu.VMEM((share // LANES, pairs * tiles, LANES), F32),
            pltpu.VMEM((pairs * tiles, share), F32),
            pltpu.VMEM((pairs * tiles, npair * pairs), BF16),
            pltpu.VMEM((WA, share), F32),
            pltpu.VMEM((tiles // WA, share), F32),
            dma,
            dma((chunks,)),
            dma((chunks,)),
            dma((chunks, ny)),
            dma((chunks, ny)),
            dma((chunks, ny - 1)),
            dma((chunks, ny - 1)),
            dma((chunks,)),
            dma((chunks,)),
            dma((5,)),
            dma((5,)),
        ],
        compiler_params=pltpu.CompilerParams(collective_id=0, has_side_effects=True),
        name="ladder_update",
    )(
        amps, amp_mask, integrals, block_mask, in_tiles, out_tiles, vir_energy,
        vir_energy.reshape(-1, 128), pair_energy, dressing,
    )


def solution(mesh):
    npair = mesh.shape["pair"]
    nz = npair // NX
    cuts = tuple(range(0, npair + 1, nz))
    in_specs = (
        P("pair", None, "int"),
        P("pair", None),
        P("pair", None, "int"),
        P("pair"),
        P(),
        P(),
        P(),
        P("pair"),
        P("pair", None),
    )
    out_specs = P("pair", None, "int")
    return jax.shard_map(
        functools.partial(shards, cuts), mesh=mesh, in_specs=in_specs, out_specs=out_specs, check_vma=False
    )
```

```python
import functools

import jax
import jax.numpy as jnp
from jax import lax
from jax.experimental import pallas as pl
from jax.experimental.pallas import tpu as pltpu
from jax.sharding import PartitionSpec as P

MESH = pl.DeviceIdType.MESH
BF16 = jnp.bfloat16
F32 = jnp.float32
WA = 4
NX = 4
LANES = 128
WINDOW = 2
Y_STEP, X_STEP = 1, 2
LAG = 2
NC = 2


def kernel(
    cuts,
    amps_hbm,
    mask_ref,
    ints_hbm,
    block_s,
    in_s,
    out_s,
    energy_s,
    energy_ref,
    pair_energy_s,
    dress_hbm,
    out_ref,
    amps_ref,
    dress_ref,
    ints,
    amps32,
    asend,
    arecv,
    rows,
    psend,
    precv,
    own,
    ysend,
    yrecv,
    dsend,
    drecv,
    gathered,
    dress,
    lhs,
    cycle,
    ladder,
    placing,
    first_energy,
    second_energy,
    ints_sem,
    amps_sem,
    dress_sem,
    a_send,
    a_recv,
    p_send,
    p_recv,
    y_send,
    y_recv,
    d_send,
    d_recv,
    g_send,
    g_recv,
):
    npair = asend.shape[0]
    pairs, tiles, share = amps_ref.shape
    nz = npair // NX
    _, _, ny, _, _, band = gathered.shape
    vt = tiles // WA
    chunks = len(cuts) - 1
    blocks = share // LANES
    n, i = lax.axis_index("pair"), lax.axis_index("int")
    z, x = lax.div(n, NX), lax.rem(n, NX)
    y, c = lax.div(i, NC), lax.rem(i, NC)

    def peer(o, sign):
        dx, zi = lax.div(o, nz), lax.rem(o, nz)
        half = lax.div(zi + 1, 2)
        dz = jnp.where(lax.rem(zi, 2) == 1, half, nz - half)
        zz = lax.rem(z + nz + sign * dz + nz, nz)
        xx = lax.rem(x + NX + sign * dx, NX)
        return zz * NX + xx

    def far_first(first, last, body):
        lax.fori_loop(first, last, lambda s, carry: body(last - 1 - (s - first), carry), 0)

    def y_peer(dy):
        return lax.rem(y + dy, ny) * NC + c

    partner = y * NC + (1 - c)

    barrier = pltpu.get_barrier_semaphore()

    def greet(s, carry):
        zi, dx = nz - 1 - lax.div(s, NX), lax.rem(s, NX)
        pl.semaphore_signal(barrier, 1, device_id={"pair": peer(dx * nz + zi, 1)}, device_id_type=MESH)
        return carry

    lax.fori_loop(0, npair - NX, greet, 0)
    for dx in range(1, NX):
        pl.semaphore_signal(barrier, 1, device_id={"pair": peer(dx * nz, 1)}, device_id_type=MESH)
    pl.semaphore_signal(barrier, 1, device_id={"int": partner}, device_id_type=MESH)
    for dy in range(1, ny):
        pl.semaphore_signal(barrier, 1, device_id={"int": y_peer(dy)}, device_id_type=MESH)

    load_amps = pltpu.make_async_copy(amps_hbm, amps_ref, amps_sem)
    load_amps.start()
    load_dress = pltpu.make_async_copy(dress_hbm, dress_ref, dress_sem)
    load_dress.start()
    load_ints = pltpu.make_async_copy(ints_hbm.at[0], ints, ints_sem)
    load_ints.start()
    load_amps.wait()

    mask_t = jnp.transpose(mask_ref[...].astype(F32))
    for p in range(pairs):
        keep = jnp.broadcast_to(mask_t[:, p : p + 1], (tiles, share)) > 0
        kept = jnp.where(keep, amps_ref[p].astype(F32), 0.0)
        for b in range(blocks):
            amps32[b, p * tiles : (p + 1) * tiles, :] = kept[:, b * LANES : (b + 1) * LANES]

    def order(o, carry):
        t = in_s[peer(o, 1)]
        for b in range(blocks):
            asend[o, :, b * LANES : (b + 1) * LANES] = amps32[b, pl.ds(t, pairs, stride=tiles), :].astype(BF16)
        return carry

    lax.fori_loop(0, npair, order, 0)
    arecv[0] = asend[0]

    pl.semaphore_wait(barrier, npair - 1 + 1 + ny - 1)

    def a_copy(k, o):
        return pltpu.make_async_remote_copy(
            asend.at[o], arecv.at[o], a_send.at[k], a_recv.at[k],
            device_id={"pair": peer(o, 1)}, device_id_type=MESH)

    def many(src, dst, ssem, rsem, k):
        first, last = max(cuts[k], 1), cuts[k + 1]
        return pltpu.make_async_remote_copy(
            src.at[pl.ds(first, last - first)], dst.at[pl.ds(first, last - first)],
            ssem.at[k], rsem.at[k], device_id={"pair": peer(1, 1)}, device_id_type=MESH)

    def send_chunk(k):
        def start_a(o, carry):
            a_copy(k, o).start()
            return carry

        far_first(max(cuts[k], 1), cuts[k + 1], start_a)

    for k in range(min(WINDOW, chunks)):
        send_chunk(k)

    piece = dress_ref.at[:, pl.ds(pl.multiple_of(i * band, band), band)]
    own_piece = pltpu.make_async_copy(piece, gathered.at[x, c, y, z], g_send.at[0])
    load_dress.wait()
    own_piece.start()
    own_piece.wait()

    def g_z_copy(dz):
        return pltpu.make_async_remote_copy(
            piece, gathered.at[x, c, y, z], g_send.at[1], g_recv.at[1],
            device_id={"pair": lax.rem(z + dz, nz) * NX + x}, device_id_type=MESH)

    def g_x_copy(dx):
        return pltpu.make_async_remote_copy(
            gathered.at[x, c], gathered.at[x, c], g_send.at[3], g_recv.at[3],
            device_id={"pair": z * NX + lax.rem(x + dx, NX)}, device_id_type=MESH)

    def g_y_copy(dy):
        return pltpu.make_async_remote_copy(
            gathered.at[x, c, y], gathered.at[x, c, y], g_send.at[2], g_recv.at[2],
            device_id={"int": y_peer(dy)}, device_id_type=MESH)

    def g_c_copy(xx):
        return pltpu.make_async_remote_copy(
            gathered.at[xx, c], gathered.at[xx, c], g_send.at[4], g_recv.at[4],
            device_id={"int": partner}, device_id_type=MESH)

    def start_gz(dz, carry):
        g_z_copy(dz).start()
        return carry

    lax.fori_loop(1, nz, start_gz, 0)

    def drain(ref, ssem, rsem):
        copy = pltpu.make_async_remote_copy(
            ref, ref, ssem, rsem, device_id={"int": partner}, device_id_type=MESH)
        copy.wait_send()
        copy.wait_recv()

    low = lax.broadcasted_iota(jnp.int32, (1, 128), 1) < 64
    count = pairs * WA
    for j in range(vt // 2):
        for ap in range(blocks):
            even = amps32[ap, pl.ds(2 * j, count, stride=vt), :]
            odd = amps32[ap, pl.ds(2 * j + 1, count, stride=vt), :]
            at = ap * count
            lhs[at : at + count, j * 128 : (j + 1) * 128] = jnp.where(
                low, even, pltpu.roll(odd, 64, 1)).astype(BF16)
            at += blocks * count
            lhs[at : at + count, j * 128 : (j + 1) * 128] = jnp.where(
                low, pltpu.roll(even, 64, 1), odd).astype(BF16)

    energies = energy_ref[...]
    turned = pltpu.roll(energies, 64, 1)
    for j in range(vt // 2):
        spread = jnp.where(low, energies[j : j + 1], turned[j : j + 1])
        second_energy[2 * j : 2 * j + 1, :] = jnp.concatenate([spread] * (share // 128), 1)
        spread = jnp.where(low, turned[j : j + 1], energies[j : j + 1])
        second_energy[2 * j + 1 : 2 * j + 2, :] = jnp.concatenate([spread] * (share // 128), 1)
    strip = lax.broadcasted_iota(jnp.int32, (1, share), 1) // 64
    for a in range(WA):
        row = jnp.zeros((1, share), F32)
        for s in range(share // 64):
            row = jnp.where(strip == s, energy_s[64 * a + i * (share // 64) + s], row)
        first_energy[a : a + 1, :] = row

    column = lax.broadcasted_iota(jnp.int32, (1, npair * pairs), 1)
    owner = lax.div(column, pairs)

    def target(o, found):
        return jnp.where(owner == o, out_s[peer(o, 1)], found)

    row = lax.fori_loop(0, npair, target, jnp.zeros_like(column)) + lax.rem(column, pairs) * tiles
    for p in range(pairs):
        own_rows = lax.broadcasted_iota(jnp.int32, (tiles, npair * pairs), 0) + p * tiles
        placing[p * tiles : (p + 1) * tiles, :] = jnp.where(own_rows == row, 1.0, 0.0).astype(BF16)

    scale = block_s[0].astype(F32)
    load_ints.wait()

    def product(r0, rn, j):
        block = ints[pl.ds(pl.multiple_of(j * share, share), share), :]
        part = lax.dot_general(
            rows[r0 : r0 + rn, :], block, (((1,), (1,)), ((), ())), preferred_element_type=F32)
        return (part * scale).astype(BF16)

    def p_copy(k, yy):
        span = pl.ds(cuts[k] * pairs, (cuts[k + 1] - cuts[k]) * pairs)
        return pltpu.make_async_remote_copy(
            psend.at[yy, span], precv.at[yy, span], p_send.at[k, yy], p_recv.at[k, yy],
            device_id={"int": partner}, device_id_type=MESH)

    def y_copy(k, dy):
        span = pl.ds(cuts[k] * pairs, (cuts[k + 1] - cuts[k]) * pairs)
        return pltpu.make_async_remote_copy(
            ysend.at[dy - 1, span], yrecv.at[dy - 1, span], y_send.at[k, dy - 1], y_recv.at[k, dy - 1],
            device_id={"int": y_peer(dy)}, device_id_type=MESH)

    def multiply(k):
        o0, o1 = cuts[k], cuts[k + 1]
        r0, rn = o0 * pairs, (o1 - o0) * pairs
        many(asend, arecv, a_send, a_recv, k).wait_recv()
        if k + WINDOW < chunks:
            send_chunk(k + WINDOW)
        rows[r0 : r0 + rn, :] = arecv[o0:o1].astype(F32).reshape(rn, share).astype(BF16)

        def for_partner(yy, carry):
            psend[yy, r0 : r0 + rn, :] = product(r0, rn, yy * NC + 1 - c)
            p_copy(k, yy).start()
            return carry

        lax.fori_loop(0, ny, for_partner, 0)

        def for_chip(step, carry):
            dy = ny - 1 - step
            yy = lax.rem(y + dy, ny)
            part = product(r0, rn, yy * NC + c).astype(F32)
            p_copy(k, yy).wait_recv()
            part = part + precv[yy, r0 : r0 + rn, :].astype(F32)

            @pl.when(dy > 0)
            def _():
                ysend[dy - 1, r0 : r0 + rn, :] = part.astype(BF16)
                y_copy(k, dy).start()

            @pl.when(dy == 0)
            def _():
                own[r0 : r0 + rn, :] = part

            return carry

        lax.fori_loop(0, ny, for_chip, 0)

    def d_copy(k, o):
        return pltpu.make_async_remote_copy(
            dsend.at[o], drecv.at[o], d_send.at[k], d_recv.at[k],
            device_id={"pair": peer(o, -1)}, device_id_type=MESH)

    def finish(k):
        o0, o1 = cuts[k], cuts[k + 1]
        r0, rn = o0 * pairs, (o1 - o0) * pairs
        total = own[r0 : r0 + rn, :]
        for dy in range(1, ny):
            y_copy(k, dy).wait_recv()
            total = total + yrecv[dy - 1, r0 : r0 + rn, :].astype(F32)
        dsend[o0:o1] = total.reshape(o1 - o0, pairs, share).astype(BF16)

        def start_d(o, carry):
            d_copy(k, o).start()
            return carry

        if o0 == 0:
            drecv[0] = dsend[0]
        far_first(max(o0, 1), o1, start_d)

    for k in range(chunks):
        multiply(k)
        if k >= LAG:
            finish(k - LAG)
        if k == Y_STEP:
            drain(gathered.at[x, c, y, pl.ds(0, nz - 1)], g_send.at[1], g_recv.at[1])
            for dy in range(1, ny):
                g_y_copy(dy).start()
        if k == X_STEP:
            drain(gathered.at[x, c, pl.ds(0, ny - 1)], g_send.at[2], g_recv.at[2])
            for dx in range(1, NX):
                g_x_copy(dx).start()
    for k in range(max(chunks - LAG, 0), chunks):
        finish(k)
    drain(gathered.at[pl.ds(0, NX - 1), c], g_send.at[3], g_recv.at[3])
    for xx in range(NX):
        g_c_copy(xx).start()
    drain(gathered.at[:, c], g_send.at[4], g_recv.at[4])
    for xx in range(NX):
        for cc in range(NC):
            for yy in range(ny):
                b = yy * NC + cc
                dress[:, xx, :, b * band : (b + 1) * band] = gathered[xx, cc, yy]
    width = dress.shape[-1]
    right = dress[...].reshape(width, width)
    result = jnp.dot(lhs[...], right, preferred_element_type=F32)
    for j in range(vt // 2):
        for ap in range(blocks):
            at = ap * count
            first = result[at : at + count, j * 128 : (j + 1) * 128]
            at += blocks * count
            last = result[at : at + count, j * 128 : (j + 1) * 128]
            cycle[ap, pl.ds(2 * j, count, stride=vt), :] = jnp.where(low, first, pltpu.roll(last, 64, 1))
            cycle[ap, pl.ds(2 * j + 1, count, stride=vt), :] = jnp.where(low, pltpu.roll(first, 64, 1), last)

    for k in range(chunks):
        o0, o1 = cuts[k], cuts[k + 1]
        many(dsend, drecv, d_send, d_recv, k).wait_recv()
        block = drecv[o0:o1].astype(F32).reshape((o1 - o0) * pairs, share).astype(BF16)
        part = jnp.dot(placing[:, o0 * pairs : o1 * pairs], block, preferred_element_type=F32)
        ladder[...] = part if k == 0 else ladder[...] + part

    def update(p, carry):
        for a in range(WA):
            at = pl.ds(pl.multiple_of(p * tiles + a * vt, vt), vt)
            below = (pair_energy_s[p] - first_energy[a : a + 1, :]) - second_energy[...]
            for b in range(blocks):
                lanes = slice(b * LANES, (b + 1) * LANES)
                value = amps32[b, at, :] + (ladder[at, lanes] + cycle[b, at, :]) / below[:, lanes]
                out_ref[p, a * vt : (a + 1) * vt, lanes] = value.astype(BF16)
        return carry

    lax.fori_loop(0, pairs, update, 0)

    for k in range(chunks):
        many(asend, arecv, a_send, a_recv, k).wait_send()
        many(dsend, drecv, d_send, d_recv, k).wait_send()
        for yy in range(ny):
            p_copy(k, yy).wait_send()
        for dy in range(1, ny):
            y_copy(k, dy).wait_send()


def shards(
    cuts, amps, amp_mask, integrals, block_mask, in_tiles, out_tiles, vir_energy, pair_energy, dressing
):
    pairs, tiles, share = amps.shape
    npair = tiles
    nz = npair // NX
    nint = integrals.shape[1] // share
    ny = nint // NC
    width = dressing.shape[1]
    chunks = len(cuts) - 1
    vmem = pl.BlockSpec(memory_space=pltpu.VMEM)
    smem = pl.BlockSpec(memory_space=pltpu.SMEM)
    hbm = pl.BlockSpec(memory_space=pl.ANY)
    dma = pltpu.SemaphoreType.DMA
    total = npair * pairs
    return pl.pallas_call(
        functools.partial(kernel, cuts),
        out_shape=jax.ShapeDtypeStruct(amps.shape, BF16),
        in_specs=[hbm, vmem, hbm, smem, smem, smem, smem, vmem, smem, hbm],
        out_specs=vmem,
        scratch_shapes=[
            pltpu.VMEM(amps.shape, BF16),
            pltpu.VMEM(dressing.shape, BF16),
            pltpu.VMEM((nint * share, share), BF16),
            pltpu.VMEM((share // LANES, pairs * tiles, LANES), F32),
            pltpu.VMEM((npair, pairs, share), BF16),
            pltpu.VMEM((npair, pairs, share), BF16),
            pltpu.VMEM((total, share), BF16),
            pltpu.VMEM((ny, total, share), BF16),
            pltpu.VMEM((ny, total, share), BF16),
            pltpu.VMEM((total, share), F32),
            pltpu.VMEM((ny - 1, total, share), BF16),
            pltpu.VMEM((ny - 1, total, share), BF16),
            pltpu.VMEM((npair, pairs, share), BF16),
            pltpu.VMEM((npair, pairs, share), BF16),
            pltpu.VMEM((NX, NC, ny, nz, dressing.shape[0], width // nint), BF16),
            pltpu.VMEM((nz, NX, dressing.shape[0], width), BF16),
            pltpu.VMEM((pairs * WA * (share // 64), width), BF16),
            pltpu.VMEM((share // LANES, pairs * tiles, LANES), F32),
            pltpu.VMEM((pairs * tiles, share), F32),
            pltpu.VMEM((pairs * tiles, npair * pairs), BF16),
            pltpu.VMEM((WA, share), F32),
            pltpu.VMEM((tiles // WA, share), F32),
            dma,
            dma,
            dma,
            dma((chunks,)),
            dma((chunks,)),
            dma((chunks, ny)),
            dma((chunks, ny)),
            dma((chunks, ny - 1)),
            dma((chunks, ny - 1)),
            dma((chunks,)),
            dma((chunks,)),
            dma((5,)),
            dma((5,)),
        ],
        compiler_params=pltpu.CompilerParams(collective_id=0, has_side_effects=True),
        name="ladder_update",
    )(
        amps, amp_mask, integrals, block_mask, in_tiles, out_tiles, vir_energy,
        vir_energy.reshape(-1, 128), pair_energy, dressing,
    )


def solution(mesh):
    npair = mesh.shape["pair"]
    nz = npair // NX
    cuts = tuple(range(0, npair + 1, nz))
    in_specs = (
        P("pair", None, "int"),
        P("pair", None),
        P("pair", None, "int"),
        P("pair"),
        P(),
        P(),
        P(),
        P("pair"),
        P("pair", None),
    )
    out_specs = P("pair", None, "int")
    return jax.shard_map(
        functools.partial(shards, cuts), mesh=mesh, in_specs=in_specs, out_specs=out_specs, check_vma=False
    )
```

```python
import functools

import jax
import jax.numpy as jnp
from jax import lax
from jax.experimental import pallas as pl
from jax.experimental.pallas import tpu as pltpu
from jax.sharding import PartitionSpec as P

MESH = pl.DeviceIdType.MESH
BF16 = jnp.bfloat16
F32 = jnp.float32
WA = 4
NX = 4
LANES = 128
WINDOW = 2
Y_STEP, X_STEP = 1, 2
LAG = 2
NC = 2


def kernel(
    cuts,
    amps_hbm,
    mask_ref,
    ints_hbm,
    block_s,
    in_s,
    out_s,
    energy_s,
    energy_ref,
    pair_energy_s,
    dress_hbm,
    out_ref,
    amps_ref,
    dress_ref,
    ints,
    amps32,
    asend,
    arecv,
    rows,
    psend,
    precv,
    own,
    ysend,
    yrecv,
    dsend,
    drecv,
    gathered,
    dress,
    lhs,
    cycle,
    ladder,
    placing,
    first_energy,
    second_energy,
    ints_sem,
    amps_sem,
    dress_sem,
    a_send,
    a_recv,
    p_send,
    p_recv,
    y_send,
    y_recv,
    d_send,
    d_recv,
    g_send,
    g_recv,
):
    npair = asend.shape[0]
    pairs, tiles, share = amps_ref.shape
    nz = npair // NX
    _, _, ny, _, _, band = gathered.shape
    vt = tiles // WA
    chunks = len(cuts) - 1
    blocks = share // LANES
    n, i = lax.axis_index("pair"), lax.axis_index("int")
    z, x = lax.div(n, NX), lax.rem(n, NX)
    y, c = lax.div(i, NC), lax.rem(i, NC)

    def peer(o, sign):
        dx, zi = lax.div(o, nz), lax.rem(o, nz)
        half = lax.div(zi + 1, 2)
        dz = jnp.where(lax.rem(zi, 2) == 1, half, nz - half)
        zz = lax.rem(z + nz + sign * dz + nz, nz)
        xx = lax.rem(x + NX + sign * dx, NX)
        return zz * NX + xx

    def far_first(first, last, body):
        lax.fori_loop(first, last, lambda s, carry: body(last - 1 - (s - first), carry), 0)

    def y_peer(dy):
        return lax.rem(y + dy, ny) * NC + c

    partner = y * NC + (1 - c)

    barrier = pltpu.get_barrier_semaphore()

    def greet(s, carry):
        zi, dx = nz - 1 - lax.div(s, NX), lax.rem(s, NX)
        pl.semaphore_signal(barrier, 1, device_id={"pair": peer(dx * nz + zi, 1)}, device_id_type=MESH)
        return carry

    lax.fori_loop(0, npair - NX, greet, 0)
    for dx in range(1, NX):
        pl.semaphore_signal(barrier, 1, device_id={"pair": peer(dx * nz, 1)}, device_id_type=MESH)
    pl.semaphore_signal(barrier, 1, device_id={"int": partner}, device_id_type=MESH)
    for dy in range(1, ny):
        pl.semaphore_signal(barrier, 1, device_id={"int": y_peer(dy)}, device_id_type=MESH)

    load_amps = pltpu.make_async_copy(amps_hbm, amps_ref, amps_sem)
    load_amps.start()
    load_dress = pltpu.make_async_copy(dress_hbm, dress_ref, dress_sem)
    load_dress.start()
    load_ints = pltpu.make_async_copy(ints_hbm.at[0], ints, ints_sem)
    load_ints.start()
    load_amps.wait()

    mask_t = jnp.transpose(mask_ref[...].astype(F32))
    for p in range(pairs):
        keep = jnp.broadcast_to(mask_t[:, p : p + 1], (tiles, share)) > 0
        kept = jnp.where(keep, amps_ref[p].astype(F32), 0.0)
        for b in range(blocks):
            amps32[b, p * tiles : (p + 1) * tiles, :] = kept[:, b * LANES : (b + 1) * LANES]

    def order(o, carry):
        t = in_s[peer(o, 1)]
        for b in range(blocks):
            asend[o, :, b * LANES : (b + 1) * LANES] = amps32[b, pl.ds(t, pairs, stride=tiles), :].astype(BF16)
        return carry

    lax.fori_loop(0, npair, order, 0)
    arecv[0] = asend[0]

    pl.semaphore_wait(barrier, npair - 1 + 1 + ny - 1)

    def a_copy(k, o):
        return pltpu.make_async_remote_copy(
            asend.at[o], arecv.at[o], a_send.at[k], a_recv.at[k],
            device_id={"pair": peer(o, 1)}, device_id_type=MESH)

    def many(src, dst, ssem, rsem, k):
        first, last = max(cuts[k], 1), cuts[k + 1]
        return pltpu.make_async_remote_copy(
            src.at[pl.ds(first, last - first)], dst.at[pl.ds(first, last - first)],
            ssem.at[k], rsem.at[k], device_id={"pair": peer(1, 1)}, device_id_type=MESH)

    def send_chunk(k):
        def start_a(o, carry):
            a_copy(k, o).start()
            return carry

        far_first(max(cuts[k], 1), cuts[k + 1], start_a)

    for k in range(min(WINDOW, chunks)):
        send_chunk(k)

    piece = dress_ref.at[:, pl.ds(pl.multiple_of(i * band, band), band)]
    own_piece = pltpu.make_async_copy(piece, gathered.at[x, c, y, z], g_send.at[0])
    load_dress.wait()
    own_piece.start()
    own_piece.wait()

    def g_z_copy(dz):
        return pltpu.make_async_remote_copy(
            piece, gathered.at[x, c, y, z], g_send.at[1], g_recv.at[1],
            device_id={"pair": lax.rem(z + dz, nz) * NX + x}, device_id_type=MESH)

    def g_x_copy(dx):
        return pltpu.make_async_remote_copy(
            gathered.at[x, c], gathered.at[x, c], g_send.at[3], g_recv.at[3],
            device_id={"pair": z * NX + lax.rem(x + dx, NX)}, device_id_type=MESH)

    def g_y_copy(dy):
        return pltpu.make_async_remote_copy(
            gathered.at[x, c, y], gathered.at[x, c, y], g_send.at[2], g_recv.at[2],
            device_id={"int": y_peer(dy)}, device_id_type=MESH)

    def g_c_copy(xx):
        return pltpu.make_async_remote_copy(
            gathered.at[xx, c], gathered.at[xx, c], g_send.at[4], g_recv.at[4],
            device_id={"int": partner}, device_id_type=MESH)

    def start_gz(dz, carry):
        g_z_copy(dz).start()
        return carry

    lax.fori_loop(1, nz, start_gz, 0)

    def drain(ref, ssem, rsem):
        copy = pltpu.make_async_remote_copy(
            ref, ref, ssem, rsem, device_id={"int": partner}, device_id_type=MESH)
        copy.wait_send()
        copy.wait_recv()

    low = lax.broadcasted_iota(jnp.int32, (1, 128), 1) < 64
    count = pairs * WA
    for j in range(vt // 2):
        for ap in range(blocks):
            even = amps32[ap, pl.ds(2 * j, count, stride=vt), :]
            odd = amps32[ap, pl.ds(2 * j + 1, count, stride=vt), :]
            at = ap * count
            lhs[at : at + count, j * 128 : (j + 1) * 128] = jnp.where(
                low, even, pltpu.roll(odd, 64, 1)).astype(BF16)
            at += blocks * count
            lhs[at : at + count, j * 128 : (j + 1) * 128] = jnp.where(
                low, pltpu.roll(even, 64, 1), odd).astype(BF16)

    energies = energy_ref[...]
    turned = pltpu.roll(energies, 64, 1)
    for j in range(vt // 2):
        spread = jnp.where(low, energies[j : j + 1], turned[j : j + 1])
        second_energy[2 * j : 2 * j + 1, :] = jnp.concatenate([spread] * (share // 128), 1)
        spread = jnp.where(low, turned[j : j + 1], energies[j : j + 1])
        second_energy[2 * j + 1 : 2 * j + 2, :] = jnp.concatenate([spread] * (share // 128), 1)
    strip = lax.broadcasted_iota(jnp.int32, (1, share), 1) // 64
    for a in range(WA):
        row = jnp.zeros((1, share), F32)
        for s in range(share // 64):
            row = jnp.where(strip == s, energy_s[64 * a + i * (share // 64) + s], row)
        first_energy[a : a + 1, :] = row

    column = lax.broadcasted_iota(jnp.int32, (1, npair * pairs), 1)
    owner = lax.div(column, pairs)

    def target(o, found):
        return jnp.where(owner == o, out_s[peer(o, 1)], found)

    row = lax.fori_loop(0, npair, target, jnp.zeros_like(column)) + lax.rem(column, pairs) * tiles
    for p in range(pairs):
        own_rows = lax.broadcasted_iota(jnp.int32, (tiles, npair * pairs), 0) + p * tiles
        placing[p * tiles : (p + 1) * tiles, :] = jnp.where(own_rows == row, 1.0, 0.0).astype(BF16)

    scale = block_s[0].astype(F32)
    load_ints.wait()

    def product(r0, rn, j):
        block = ints[pl.ds(pl.multiple_of(j * share, share), share), :]
        part = lax.dot_general(
            rows[r0 : r0 + rn, :], block, (((1,), (1,)), ((), ())), preferred_element_type=F32)
        return (part * scale).astype(BF16)

    def p_copy(k, yy):
        span = pl.ds(cuts[k] * pairs, (cuts[k + 1] - cuts[k]) * pairs)
        return pltpu.make_async_remote_copy(
            psend.at[yy, span], precv.at[yy, span], p_send.at[k, yy], p_recv.at[k, yy],
            device_id={"int": partner}, device_id_type=MESH)

    def y_copy(k, dy):
        span = pl.ds(cuts[k] * pairs, (cuts[k + 1] - cuts[k]) * pairs)
        return pltpu.make_async_remote_copy(
            ysend.at[dy - 1, span], yrecv.at[dy - 1, span], y_send.at[k, dy - 1], y_recv.at[k, dy - 1],
            device_id={"int": y_peer(dy)}, device_id_type=MESH)

    def multiply(k):
        o0, o1 = cuts[k], cuts[k + 1]
        r0, rn = o0 * pairs, (o1 - o0) * pairs
        many(asend, arecv, a_send, a_recv, k).wait_recv()
        if k + WINDOW < chunks:
            send_chunk(k + WINDOW)
        rows[r0 : r0 + rn, :] = arecv[o0:o1].astype(F32).reshape(rn, share).astype(BF16)

        def for_partner(step, carry):
            yy = lax.rem(y + ny - 1 - step, ny)
            psend[yy, r0 : r0 + rn, :] = product(r0, rn, yy * NC + 1 - c)
            p_copy(k, yy).start()
            return carry

        lax.fori_loop(0, ny, for_partner, 0)

        def for_chip(step, carry):
            dy = ny - 1 - step
            yy = lax.rem(y + dy, ny)
            part = product(r0, rn, yy * NC + c).astype(F32)
            p_copy(k, yy).wait_recv()
            part = part + precv[yy, r0 : r0 + rn, :].astype(F32)

            @pl.when(dy > 0)
            def _():
                ysend[dy - 1, r0 : r0 + rn, :] = part.astype(BF16)
                y_copy(k, dy).start()

            @pl.when(dy == 0)
            def _():
                own[r0 : r0 + rn, :] = part

            return carry

        lax.fori_loop(0, ny, for_chip, 0)

    def d_copy(k, o):
        return pltpu.make_async_remote_copy(
            dsend.at[o], drecv.at[o], d_send.at[k], d_recv.at[k],
            device_id={"pair": peer(o, -1)}, device_id_type=MESH)

    def finish(k):
        o0, o1 = cuts[k], cuts[k + 1]
        r0, rn = o0 * pairs, (o1 - o0) * pairs
        total = own[r0 : r0 + rn, :]
        for dy in range(1, ny):
            y_copy(k, dy).wait_recv()
            total = total + yrecv[dy - 1, r0 : r0 + rn, :].astype(F32)
        dsend[o0:o1] = total.reshape(o1 - o0, pairs, share).astype(BF16)

        def start_d(o, carry):
            d_copy(k, o).start()
            return carry

        if o0 == 0:
            drecv[0] = dsend[0]
        far_first(max(o0, 1), o1, start_d)

    for k in range(chunks):
        multiply(k)
        if k >= LAG:
            finish(k - LAG)
        if k == Y_STEP:
            drain(gathered.at[x, c, y, pl.ds(0, nz - 1)], g_send.at[1], g_recv.at[1])
            for dy in range(1, ny):
                g_y_copy(dy).start()
        if k == X_STEP:
            drain(gathered.at[x, c, pl.ds(0, ny - 1)], g_send.at[2], g_recv.at[2])
            for dx in range(1, NX):
                g_x_copy(dx).start()
    for k in range(max(chunks - LAG, 0), chunks):
        finish(k)
    drain(gathered.at[pl.ds(0, NX - 1), c], g_send.at[3], g_recv.at[3])
    for xx in range(NX):
        g_c_copy(xx).start()
    drain(gathered.at[:, c], g_send.at[4], g_recv.at[4])
    for xx in range(NX):
        for cc in range(NC):
            for yy in range(ny):
                b = yy * NC + cc
                dress[:, xx, :, b * band : (b + 1) * band] = gathered[xx, cc, yy]
    width = dress.shape[-1]
    right = dress[...].reshape(width, width)
    result = jnp.dot(lhs[...], right, preferred_element_type=F32)
    for j in range(vt // 2):
        for ap in range(blocks):
            at = ap * count
            first = result[at : at + count, j * 128 : (j + 1) * 128]
            at += blocks * count
            last = result[at : at + count, j * 128 : (j + 1) * 128]
            cycle[ap, pl.ds(2 * j, count, stride=vt), :] = jnp.where(low, first, pltpu.roll(last, 64, 1))
            cycle[ap, pl.ds(2 * j + 1, count, stride=vt), :] = jnp.where(low, pltpu.roll(first, 64, 1), last)

    for k in range(chunks):
        o0, o1 = cuts[k], cuts[k + 1]
        many(dsend, drecv, d_send, d_recv, k).wait_recv()
        block = drecv[o0:o1].astype(F32).reshape((o1 - o0) * pairs, share).astype(BF16)
        part = jnp.dot(placing[:, o0 * pairs : o1 * pairs], block, preferred_element_type=F32)
        ladder[...] = part if k == 0 else ladder[...] + part

    def update(p, carry):
        for a in range(WA):
            at = pl.ds(pl.multiple_of(p * tiles + a * vt, vt), vt)
            below = (pair_energy_s[p] - first_energy[a : a + 1, :]) - second_energy[...]
            for b in range(blocks):
                lanes = slice(b * LANES, (b + 1) * LANES)
                value = amps32[b, at, :] + (ladder[at, lanes] + cycle[b, at, :]) / below[:, lanes]
                out_ref[p, a * vt : (a + 1) * vt, lanes] = value.astype(BF16)
        return carry

    lax.fori_loop(0, pairs, update, 0)

    for k in range(chunks):
        many(asend, arecv, a_send, a_recv, k).wait_send()
        many(dsend, drecv, d_send, d_recv, k).wait_send()
        for yy in range(ny):
            p_copy(k, yy).wait_send()
        for dy in range(1, ny):
            y_copy(k, dy).wait_send()


def shards(
    cuts, amps, amp_mask, integrals, block_mask, in_tiles, out_tiles, vir_energy, pair_energy, dressing
):
    pairs, tiles, share = amps.shape
    npair = tiles
    nz = npair // NX
    nint = integrals.shape[1] // share
    ny = nint // NC
    width = dressing.shape[1]
    chunks = len(cuts) - 1
    vmem = pl.BlockSpec(memory_space=pltpu.VMEM)
    smem = pl.BlockSpec(memory_space=pltpu.SMEM)
    hbm = pl.BlockSpec(memory_space=pl.ANY)
    dma = pltpu.SemaphoreType.DMA
    total = npair * pairs
    return pl.pallas_call(
        functools.partial(kernel, cuts),
        out_shape=jax.ShapeDtypeStruct(amps.shape, BF16),
        in_specs=[hbm, vmem, hbm, smem, smem, smem, smem, vmem, smem, hbm],
        out_specs=vmem,
        scratch_shapes=[
            pltpu.VMEM(amps.shape, BF16),
            pltpu.VMEM(dressing.shape, BF16),
            pltpu.VMEM((nint * share, share), BF16),
            pltpu.VMEM((share // LANES, pairs * tiles, LANES), F32),
            pltpu.VMEM((npair, pairs, share), BF16),
            pltpu.VMEM((npair, pairs, share), BF16),
            pltpu.VMEM((total, share), BF16),
            pltpu.VMEM((ny, total, share), BF16),
            pltpu.VMEM((ny, total, share), BF16),
            pltpu.VMEM((total, share), F32),
            pltpu.VMEM((ny - 1, total, share), BF16),
            pltpu.VMEM((ny - 1, total, share), BF16),
            pltpu.VMEM((npair, pairs, share), BF16),
            pltpu.VMEM((npair, pairs, share), BF16),
            pltpu.VMEM((NX, NC, ny, nz, dressing.shape[0], width // nint), BF16),
            pltpu.VMEM((nz, NX, dressing.shape[0], width), BF16),
            pltpu.VMEM((pairs * WA * (share // 64), width), BF16),
            pltpu.VMEM((share // LANES, pairs * tiles, LANES), F32),
            pltpu.VMEM((pairs * tiles, share), F32),
            pltpu.VMEM((pairs * tiles, npair * pairs), BF16),
            pltpu.VMEM((WA, share), F32),
            pltpu.VMEM((tiles // WA, share), F32),
            dma,
            dma,
            dma,
            dma((chunks,)),
            dma((chunks,)),
            dma((chunks, ny)),
            dma((chunks, ny)),
            dma((chunks, ny - 1)),
            dma((chunks, ny - 1)),
            dma((chunks,)),
            dma((chunks,)),
            dma((5,)),
            dma((5,)),
        ],
        compiler_params=pltpu.CompilerParams(collective_id=0, has_side_effects=True),
        name="ladder_update",
    )(
        amps, amp_mask, integrals, block_mask, in_tiles, out_tiles, vir_energy,
        vir_energy.reshape(-1, 128), pair_energy, dressing,
    )


def solution(mesh):
    npair = mesh.shape["pair"]
    nz = npair // NX
    cuts = tuple(range(0, npair + 1, nz))
    in_specs = (
        P("pair", None, "int"),
        P("pair", None),
        P("pair", None, "int"),
        P("pair"),
        P(),
        P(),
        P(),
        P("pair"),
        P("pair", None),
    )
    out_specs = P("pair", None, "int")
    return jax.shard_map(
        functools.partial(shards, cuts), mesh=mesh, in_specs=in_specs, out_specs=out_specs, check_vma=False
    )
```

```python
import functools

import jax
import jax.numpy as jnp
from jax import lax
from jax.experimental import pallas as pl
from jax.experimental.pallas import tpu as pltpu
from jax.sharding import PartitionSpec as P

MESH = pl.DeviceIdType.MESH
BF16 = jnp.bfloat16
F32 = jnp.float32
WA = 4
NX = 4
LANES = 128
WINDOW = 2
Y_STEP, X_STEP = 1, 2
LAG = 2
NC = 2


def kernel(
    cuts,
    amps_hbm,
    mask_ref,
    ints_hbm,
    block_s,
    in_s,
    out_s,
    energy_s,
    energy_ref,
    pair_energy_s,
    dress_hbm,
    out_ref,
    amps_ref,
    dress_ref,
    ints,
    amps32,
    asend,
    arecv,
    rows,
    psend,
    precv,
    own,
    ysend,
    yrecv,
    dsend,
    drecv,
    gathered,
    dress,
    lhs,
    cycle,
    ladder,
    placing,
    first_energy,
    second_energy,
    ints_sem,
    amps_sem,
    dress_sem,
    a_send,
    a_recv,
    p_send,
    p_recv,
    y_send,
    y_recv,
    d_send,
    d_recv,
    g_send,
    g_recv,
):
    npair = asend.shape[0]
    pairs, tiles, share = amps_ref.shape
    nz = npair // NX
    _, _, ny, _, _, band = gathered.shape
    vt = tiles // WA
    chunks = len(cuts) - 1
    blocks = share // LANES
    n, i = lax.axis_index("pair"), lax.axis_index("int")
    z, x = lax.div(n, NX), lax.rem(n, NX)
    y, c = lax.div(i, NC), lax.rem(i, NC)

    def peer(o, sign):
        dx, zi = lax.div(o, nz), lax.rem(o, nz)
        half = lax.div(zi + 1, 2)
        dz = jnp.where(lax.rem(zi, 2) == 1, half, nz - half)
        zz = lax.rem(z + nz + sign * dz + nz, nz)
        xx = lax.rem(x + NX + sign * dx, NX)
        return zz * NX + xx

    def far_first(first, last, body):
        lax.fori_loop(first, last, lambda s, carry: body(last - 1 - (s - first), carry), 0)

    def y_peer(dy):
        return lax.rem(y + dy, ny) * NC + c

    def turn(step):
        dy = ny - 1 - step
        return jnp.where(dy == ny - 1, ny // 2, jnp.where(dy == ny // 2, ny - 1, dy))

    partner = y * NC + (1 - c)

    barrier = pltpu.get_barrier_semaphore()

    def greet(s, carry):
        zi, dx = nz - 1 - lax.div(s, NX), lax.rem(s, NX)
        pl.semaphore_signal(barrier, 1, device_id={"pair": peer(dx * nz + zi, 1)}, device_id_type=MESH)
        return carry

    lax.fori_loop(0, npair - NX, greet, 0)
    for dx in range(1, NX):
        pl.semaphore_signal(barrier, 1, device_id={"pair": peer(dx * nz, 1)}, device_id_type=MESH)
    pl.semaphore_signal(barrier, 1, device_id={"int": partner}, device_id_type=MESH)
    for dy in range(1, ny):
        pl.semaphore_signal(barrier, 1, device_id={"int": y_peer(dy)}, device_id_type=MESH)

    load_amps = pltpu.make_async_copy(amps_hbm, amps_ref, amps_sem)
    load_amps.start()
    load_dress = pltpu.make_async_copy(dress_hbm, dress_ref, dress_sem)
    load_dress.start()
    load_ints = pltpu.make_async_copy(ints_hbm.at[0], ints, ints_sem)
    load_ints.start()
    load_amps.wait()

    mask_t = jnp.transpose(mask_ref[...].astype(F32))
    for p in range(pairs):
        keep = jnp.broadcast_to(mask_t[:, p : p + 1], (tiles, share)) > 0
        kept = jnp.where(keep, amps_ref[p].astype(F32), 0.0)
        for b in range(blocks):
            amps32[b, p * tiles : (p + 1) * tiles, :] = kept[:, b * LANES : (b + 1) * LANES]

    def order(o, carry):
        t = in_s[peer(o, 1)]
        for b in range(blocks):
            asend[o, :, b * LANES : (b + 1) * LANES] = amps32[b, pl.ds(t, pairs, stride=tiles), :].astype(BF16)
        return carry

    lax.fori_loop(0, npair, order, 0)
    arecv[0] = asend[0]

    pl.semaphore_wait(barrier, npair - 1 + 1 + ny - 1)

    def a_copy(k, o):
        return pltpu.make_async_remote_copy(
            asend.at[o], arecv.at[o], a_send.at[k], a_recv.at[k],
            device_id={"pair": peer(o, 1)}, device_id_type=MESH)

    def many(src, dst, ssem, rsem, k):
        first, last = max(cuts[k], 1), cuts[k + 1]
        return pltpu.make_async_remote_copy(
            src.at[pl.ds(first, last - first)], dst.at[pl.ds(first, last - first)],
            ssem.at[k], rsem.at[k], device_id={"pair": peer(1, 1)}, device_id_type=MESH)

    def send_chunk(k):
        def start_a(o, carry):
            a_copy(k, o).start()
            return carry

        far_first(max(cuts[k], 1), cuts[k + 1], start_a)

    for k in range(min(WINDOW, chunks)):
        send_chunk(k)

    piece = dress_ref.at[:, pl.ds(pl.multiple_of(i * band, band), band)]
    own_piece = pltpu.make_async_copy(piece, gathered.at[x, c, y, z], g_send.at[0])
    load_dress.wait()
    own_piece.start()
    own_piece.wait()

    def g_z_copy(dz):
        return pltpu.make_async_remote_copy(
            piece, gathered.at[x, c, y, z], g_send.at[1], g_recv.at[1],
            device_id={"pair": lax.rem(z + dz, nz) * NX + x}, device_id_type=MESH)

    def g_x_copy(dx):
        return pltpu.make_async_remote_copy(
            gathered.at[x, c], gathered.at[x, c], g_send.at[3], g_recv.at[3],
            device_id={"pair": z * NX + lax.rem(x + dx, NX)}, device_id_type=MESH)

    def g_y_copy(dy):
        return pltpu.make_async_remote_copy(
            gathered.at[x, c, y], gathered.at[x, c, y], g_send.at[2], g_recv.at[2],
            device_id={"int": y_peer(dy)}, device_id_type=MESH)

    def g_c_copy(xx):
        return pltpu.make_async_remote_copy(
            gathered.at[xx, c], gathered.at[xx, c], g_send.at[4], g_recv.at[4],
            device_id={"int": partner}, device_id_type=MESH)

    def start_gz(dz, carry):
        g_z_copy(dz).start()
        return carry

    lax.fori_loop(1, nz, start_gz, 0)

    def drain(ref, ssem, rsem):
        copy = pltpu.make_async_remote_copy(
            ref, ref, ssem, rsem, device_id={"int": partner}, device_id_type=MESH)
        copy.wait_send()
        copy.wait_recv()

    low = lax.broadcasted_iota(jnp.int32, (1, 128), 1) < 64
    count = pairs * WA
    for j in range(vt // 2):
        for ap in range(blocks):
            even = amps32[ap, pl.ds(2 * j, count, stride=vt), :]
            odd = amps32[ap, pl.ds(2 * j + 1, count, stride=vt), :]
            at = ap * count
            lhs[at : at + count, j * 128 : (j + 1) * 128] = jnp.where(
                low, even, pltpu.roll(odd, 64, 1)).astype(BF16)
            at += blocks * count
            lhs[at : at + count, j * 128 : (j + 1) * 128] = jnp.where(
                low, pltpu.roll(even, 64, 1), odd).astype(BF16)

    energies = energy_ref[...]
    turned = pltpu.roll(energies, 64, 1)
    for j in range(vt // 2):
        spread = jnp.where(low, energies[j : j + 1], turned[j : j + 1])
        second_energy[2 * j : 2 * j + 1, :] = jnp.concatenate([spread] * (share // 128), 1)
        spread = jnp.where(low, turned[j : j + 1], energies[j : j + 1])
        second_energy[2 * j + 1 : 2 * j + 2, :] = jnp.concatenate([spread] * (share // 128), 1)
    strip = lax.broadcasted_iota(jnp.int32, (1, share), 1) // 64
    for a in range(WA):
        row = jnp.zeros((1, share), F32)
        for s in range(share // 64):
            row = jnp.where(strip == s, energy_s[64 * a + i * (share // 64) + s], row)
        first_energy[a : a + 1, :] = row

    column = lax.broadcasted_iota(jnp.int32, (1, npair * pairs), 1)
    owner = lax.div(column, pairs)

    def target(o, found):
        return jnp.where(owner == o, out_s[peer(o, 1)], found)

    row = lax.fori_loop(0, npair, target, jnp.zeros_like(column)) + lax.rem(column, pairs) * tiles
    for p in range(pairs):
        own_rows = lax.broadcasted_iota(jnp.int32, (tiles, npair * pairs), 0) + p * tiles
        placing[p * tiles : (p + 1) * tiles, :] = jnp.where(own_rows == row, 1.0, 0.0).astype(BF16)

    scale = block_s[0].astype(F32)
    load_ints.wait()

    def product(r0, rn, j):
        block = ints[pl.ds(pl.multiple_of(j * share, share), share), :]
        part = lax.dot_general(
            rows[r0 : r0 + rn, :], block, (((1,), (1,)), ((), ())), preferred_element_type=F32)
        return (part * scale).astype(BF16)

    def p_copy(k, yy):
        span = pl.ds(cuts[k] * pairs, (cuts[k + 1] - cuts[k]) * pairs)
        return pltpu.make_async_remote_copy(
            psend.at[yy, span], precv.at[yy, span], p_send.at[k, yy], p_recv.at[k, yy],
            device_id={"int": partner}, device_id_type=MESH)

    def y_copy(k, dy):
        span = pl.ds(cuts[k] * pairs, (cuts[k + 1] - cuts[k]) * pairs)
        return pltpu.make_async_remote_copy(
            ysend.at[dy - 1, span], yrecv.at[dy - 1, span], y_send.at[k, dy - 1], y_recv.at[k, dy - 1],
            device_id={"int": y_peer(dy)}, device_id_type=MESH)

    def multiply(k):
        o0, o1 = cuts[k], cuts[k + 1]
        r0, rn = o0 * pairs, (o1 - o0) * pairs
        many(asend, arecv, a_send, a_recv, k).wait_recv()
        if k + WINDOW < chunks:
            send_chunk(k + WINDOW)
        rows[r0 : r0 + rn, :] = arecv[o0:o1].astype(F32).reshape(rn, share).astype(BF16)

        def for_partner(step, carry):
            yy = lax.rem(y + turn(step), ny)
            psend[yy, r0 : r0 + rn, :] = product(r0, rn, yy * NC + 1 - c)
            p_copy(k, yy).start()
            return carry

        lax.fori_loop(0, ny, for_partner, 0)

        def for_chip(step, carry):
            dy = turn(step)
            yy = lax.rem(y + dy, ny)
            part = product(r0, rn, yy * NC + c).astype(F32)
            p_copy(k, yy).wait_recv()
            part = part + precv[yy, r0 : r0 + rn, :].astype(F32)

            @pl.when(dy > 0)
            def _():
                ysend[dy - 1, r0 : r0 + rn, :] = part.astype(BF16)
                y_copy(k, dy).start()

            @pl.when(dy == 0)
            def _():
                own[r0 : r0 + rn, :] = part

            return carry

        lax.fori_loop(0, ny, for_chip, 0)

    def d_copy(k, o):
        return pltpu.make_async_remote_copy(
            dsend.at[o], drecv.at[o], d_send.at[k], d_recv.at[k],
            device_id={"pair": peer(o, -1)}, device_id_type=MESH)

    def finish(k):
        o0, o1 = cuts[k], cuts[k + 1]
        r0, rn = o0 * pairs, (o1 - o0) * pairs
        total = own[r0 : r0 + rn, :]
        for dy in range(1, ny):
            y_copy(k, dy).wait_recv()
            total = total + yrecv[dy - 1, r0 : r0 + rn, :].astype(F32)
        dsend[o0:o1] = total.reshape(o1 - o0, pairs, share).astype(BF16)

        def start_d(o, carry):
            d_copy(k, o).start()
            return carry

        if o0 == 0:
            drecv[0] = dsend[0]
        far_first(max(o0, 1), o1, start_d)

    for k in range(chunks):
        multiply(k)
        if k >= LAG:
            finish(k - LAG)
        if k == Y_STEP:
            drain(gathered.at[x, c, y, pl.ds(0, nz - 1)], g_send.at[1], g_recv.at[1])
            for dy in range(1, ny):
                g_y_copy(dy).start()
        if k == X_STEP:
            drain(gathered.at[x, c, pl.ds(0, ny - 1)], g_send.at[2], g_recv.at[2])
            for dx in range(1, NX):
                g_x_copy(dx).start()
    for k in range(max(chunks - LAG, 0), chunks):
        finish(k)
    drain(gathered.at[pl.ds(0, NX - 1), c], g_send.at[3], g_recv.at[3])
    for xx in range(NX):
        g_c_copy(xx).start()
    drain(gathered.at[:, c], g_send.at[4], g_recv.at[4])
    for xx in range(NX):
        for cc in range(NC):
            for yy in range(ny):
                b = yy * NC + cc
                dress[:, xx, :, b * band : (b + 1) * band] = gathered[xx, cc, yy]
    width = dress.shape[-1]
    right = dress[...].reshape(width, width)
    result = jnp.dot(lhs[...], right, preferred_element_type=F32)
    for j in range(vt // 2):
        for ap in range(blocks):
            at = ap * count
            first = result[at : at + count, j * 128 : (j + 1) * 128]
            at += blocks * count
            last = result[at : at + count, j * 128 : (j + 1) * 128]
            cycle[ap, pl.ds(2 * j, count, stride=vt), :] = jnp.where(low, first, pltpu.roll(last, 64, 1))
            cycle[ap, pl.ds(2 * j + 1, count, stride=vt), :] = jnp.where(low, pltpu.roll(first, 64, 1), last)

    for k in range(chunks):
        o0, o1 = cuts[k], cuts[k + 1]
        many(dsend, drecv, d_send, d_recv, k).wait_recv()
        block = drecv[o0:o1].astype(F32).reshape((o1 - o0) * pairs, share).astype(BF16)
        part = jnp.dot(placing[:, o0 * pairs : o1 * pairs], block, preferred_element_type=F32)
        ladder[...] = part if k == 0 else ladder[...] + part

    def update(p, carry):
        for a in range(WA):
            at = pl.ds(pl.multiple_of(p * tiles + a * vt, vt), vt)
            below = (pair_energy_s[p] - first_energy[a : a + 1, :]) - second_energy[...]
            for b in range(blocks):
                lanes = slice(b * LANES, (b + 1) * LANES)
                value = amps32[b, at, :] + (ladder[at, lanes] + cycle[b, at, :]) / below[:, lanes]
                out_ref[p, a * vt : (a + 1) * vt, lanes] = value.astype(BF16)
        return carry

    lax.fori_loop(0, pairs, update, 0)

    for k in range(chunks):
        many(asend, arecv, a_send, a_recv, k).wait_send()
        many(dsend, drecv, d_send, d_recv, k).wait_send()
        for yy in range(ny):
            p_copy(k, yy).wait_send()
        for dy in range(1, ny):
            y_copy(k, dy).wait_send()


def shards(
    cuts, amps, amp_mask, integrals, block_mask, in_tiles, out_tiles, vir_energy, pair_energy, dressing
):
    pairs, tiles, share = amps.shape
    npair = tiles
    nz = npair // NX
    nint = integrals.shape[1] // share
    ny = nint // NC
    width = dressing.shape[1]
    chunks = len(cuts) - 1
    vmem = pl.BlockSpec(memory_space=pltpu.VMEM)
    smem = pl.BlockSpec(memory_space=pltpu.SMEM)
    hbm = pl.BlockSpec(memory_space=pl.ANY)
    dma = pltpu.SemaphoreType.DMA
    total = npair * pairs
    return pl.pallas_call(
        functools.partial(kernel, cuts),
        out_shape=jax.ShapeDtypeStruct(amps.shape, BF16),
        in_specs=[hbm, vmem, hbm, smem, smem, smem, smem, vmem, smem, hbm],
        out_specs=vmem,
        scratch_shapes=[
            pltpu.VMEM(amps.shape, BF16),
            pltpu.VMEM(dressing.shape, BF16),
            pltpu.VMEM((nint * share, share), BF16),
            pltpu.VMEM((share // LANES, pairs * tiles, LANES), F32),
            pltpu.VMEM((npair, pairs, share), BF16),
            pltpu.VMEM((npair, pairs, share), BF16),
            pltpu.VMEM((total, share), BF16),
            pltpu.VMEM((ny, total, share), BF16),
            pltpu.VMEM((ny, total, share), BF16),
            pltpu.VMEM((total, share), F32),
            pltpu.VMEM((ny - 1, total, share), BF16),
            pltpu.VMEM((ny - 1, total, share), BF16),
            pltpu.VMEM((npair, pairs, share), BF16),
            pltpu.VMEM((npair, pairs, share), BF16),
            pltpu.VMEM((NX, NC, ny, nz, dressing.shape[0], width // nint), BF16),
            pltpu.VMEM((nz, NX, dressing.shape[0], width), BF16),
            pltpu.VMEM((pairs * WA * (share // 64), width), BF16),
            pltpu.VMEM((share // LANES, pairs * tiles, LANES), F32),
            pltpu.VMEM((pairs * tiles, share), F32),
            pltpu.VMEM((pairs * tiles, npair * pairs), BF16),
            pltpu.VMEM((WA, share), F32),
            pltpu.VMEM((tiles // WA, share), F32),
            dma,
            dma,
            dma,
            dma((chunks,)),
            dma((chunks,)),
            dma((chunks, ny)),
            dma((chunks, ny)),
            dma((chunks, ny - 1)),
            dma((chunks, ny - 1)),
            dma((chunks,)),
            dma((chunks,)),
            dma((5,)),
            dma((5,)),
        ],
        compiler_params=pltpu.CompilerParams(collective_id=0, has_side_effects=True),
        name="ladder_update",
    )(
        amps, amp_mask, integrals, block_mask, in_tiles, out_tiles, vir_energy,
        vir_energy.reshape(-1, 128), pair_energy, dressing,
    )


def solution(mesh):
    npair = mesh.shape["pair"]
    nz = npair // NX
    cuts = tuple(range(0, npair + 1, nz))
    in_specs = (
        P("pair", None, "int"),
        P("pair", None),
        P("pair", None, "int"),
        P("pair"),
        P(),
        P(),
        P(),
        P("pair"),
        P("pair", None),
    )
    out_specs = P("pair", None, "int")
    return jax.shard_map(
        functools.partial(shards, cuts), mesh=mesh, in_specs=in_specs, out_specs=out_specs, check_vma=False
    )
```
